32 devices in a mesh: fft: 16 (over z, y, x), grp: 2 (over core).
Axes of the slice: x: 2, y: 2, z: 4, core: 2. Of those that a mesh axis runs over, the one named last changes fastest.
Arguments:
- potential: float32 [4, 256, 256, 256], P(None, 'fft', 'grp'), may hold values from -6 to 6
- stick_mill: int32 [2, 256], replicated, may hold values from -128 to 127, as said below
- positions: int32 [3, 256], P(None, 'grp'), may hold values from 0 to 255
- aug_charge: bfloat16 [171, 256, 256], P(None, 'fft'), may hold values from -0.0234375 to 0.0234375
Outputs:
- vg_sticks: float32 [4, 2, 256, 256], P(None, None, 'fft')
- d_matrix: float32 [4, 171, 256], P(None, None, 'grp')
The draws below stay inside these ranges and needn't reach their ends.
Inputs may be any that keep to these rules, and one draw needn't show every extreme that they name: `stick_mill`: stick k is owned by fft index k // 16; no two sticks have the same (gx, gy), and every stick has gx^2 + gy^2 < 128^2.
All inputs are finite; a program needn't handle non-finite values.
Results may differ from the reference program's by a relative error of at most 0.0029.
Values sent between devices are 32-bit elements; how exact they have to be, the bound alone decides.
A program may use at most 128 MiB of HBM per device.

```python
import math
import jax
import jax.numpy as jnp
from jax import lax

N = 256
SPINS = 4
PAIRS = 171
ATM_GRP = 128
STICKS = 256
ATOMS = 256
N_GRP = 2


def draw_stick_mill(key, part):
    shuffled = jax.random.permutation(jax.random.fold_in(key, 7), N * N).astype(jnp.int32)
    col_gx = shuffled // N - N // 2
    col_gy = jnp.mod(shuffled, N) - N // 2
    outside = (col_gx * col_gx + col_gy * col_gy >= N // 2 * (N // 2)).astype(jnp.int32)
    priority = jnp.arange(N * N, dtype=jnp.int32) + outside * (N * N)
    ranking = jnp.argsort(priority, stable=True)[:STICKS]
    chosen = shuffled[ranking]
    return jnp.stack([chosen // N - N // 2, jnp.mod(chosen, N) - N // 2]).astype(jnp.int32)


def with_ends(array, key, low, high):
    longest = array.shape.index(max(array.shape))
    spots = []
    for shift in (0, 1):
        where = [jax.random.randint(jax.random.fold_in(key, axis), (), 0, length) for axis, length in enumerate(array.shape)]
        where[longest] = (where[longest] + shift) % array.shape[longest]
        spots.append(tuple(where))
    return array.at[spots[0]].set(low).at[spots[1]].set(high)


def level_of(key, shape, shards, least, top_value):
    gain = 1.0
    for dim, blocks in shards:
        heights = jax.random.uniform(jax.random.fold_in(jax.random.fold_in(key, 6), dim), (blocks,), jnp.float32, least / len(shards), top_value / len(shards))
        gain = gain * jnp.repeat(jnp.exp(heights), shape[dim] // blocks).reshape((-1,) + (1,) * (len(shape) - 1 - dim))
    return gain


def normal_values(rng, dims, scale, most, split=(), kind=jnp.bfloat16):
    gain = level_of(rng, dims, split, -0.22, 0.18) if split else 1.0
    values = jax.random.normal(rng, dims, jnp.float32) * scale * gain
    return jnp.minimum(jnp.maximum(values, -most), most).astype(kind)


def setup_inputs(seed: int = 0) -> dict:
    key_of = jax.random.split(jax.random.key(seed), 5)
    return {
        "potential": normal_values(key_of[0], (SPINS, N, N, N), 1.0, 6.0, ((1, 16), (2, 2)), jnp.float32),
        "stick_mill": draw_stick_mill(jax.random.fold_in(key_of[4], 71), 0),
        "positions": with_ends(jax.random.randint(key_of[2], (3, ATOMS), 0, N), jax.random.fold_in(key_of[2], 1), 0, N - 1).astype(jnp.int32),
        "aug_charge": normal_values(key_of[3], (PAIRS, STICKS, N), (STICKS * N) ** -0.5, 0.0234375, ((1, 16),)),
    }


two_pi = 2.0 * math.pi


def reference(potential, stick_mill, positions, aug_charge):
    norm_factor = float(N) ** -1.5
    spectrum = jnp.fft.fftn(potential, axes=(1, 2, 3))
    grid_index = jnp.arange(N, dtype=jnp.int32)
    shifted = grid_index - N // 2
    plane_index = jnp.mod(shifted, N)
    row_index = jnp.mod(stick_mill[1], N)
    col_index = jnp.mod(stick_mill[0], N)
    picked = spectrum[:, plane_index[None, :], row_index[:, None], col_index[:, None]]
    vg_sticks = (jnp.stack([jnp.real(picked), jnp.imag(picked)], axis=1) * norm_factor).astype(jnp.float32)
    charge = aug_charge.astype(jnp.float32).reshape(PAIRS, STICKS * N)
    pos_blocks = positions.reshape(3, N_GRP, ATM_GRP).transpose(1, 0, 2)

    def atom_block(pos_group):
        phase_k = jnp.mod(stick_mill[0][:, None, None] * pos_group[0][None, None, :]
                          + stick_mill[1][:, None, None] * pos_group[1][None, None, :]
                          + shifted[None, :, None] * pos_group[2][None, None, :], N)
        angle_all = (two_pi / N) * phase_k.astype(jnp.float32)
        cosine = jnp.cos(angle_all)
        sine = jnp.sin(angle_all)
        results = []
        for channel in range(SPINS):
            mixed_term = vg_sticks[channel, 0][:, :, None] * cosine - vg_sticks[channel, 1][:, :, None] * sine
            rounded = lax.optimization_barrier(mixed_term.astype(jnp.bfloat16)).astype(jnp.float32)
            results.append(jnp.dot(charge, rounded.reshape(STICKS * N, ATM_GRP),
                                   precision=lax.Precision.HIGHEST, preferred_element_type=jnp.float32))
        return jnp.stack(results)

    blocks_out = lax.map(atom_block, pos_blocks)
    d_matrix = blocks_out.transpose(1, 2, 0, 3).reshape(SPINS, PAIRS, ATOMS)
    return vg_sticks, d_matrix
```

```python
import functools
import math

import jax
import jax.numpy as jnp
from jax import lax
from jax.experimental import pallas as pl
from jax.experimental.pallas import tpu as pltpu
from jax.sharding import PartitionSpec as P

MESH = pl.DeviceIdType.MESH
F32 = jnp.float32
BF16 = jnp.bfloat16


def cos_sin(k, n):
    quarter = n // 4
    moved = k + n // 8
    m = jnp.bitwise_and(moved, quarter - 1) - n // 8
    q = jnp.bitwise_and(jnp.right_shift(moved, quarter.bit_length() - 1), 3)
    a = m.astype(F32) * (2.0 * math.pi / n)
    b = a * a
    s = a * (1.0 + b * (-1.0 / 6 + b * (1.0 / 120 + b * (-1.0 / 5040 + b * (1.0 / 362880)))))
    c = 1.0 + b * (-0.5 + b * (1.0 / 24 + b * (-1.0 / 720 + b * (1.0 / 40320))))
    odd = jnp.bitwise_and(q, 1) == 1
    cc = jnp.where(odd, s, c)
    ss = jnp.where(odd, c, s)
    cc = jnp.where((q == 1) | (q == 2), -cc, cc)
    ss = jnp.where(q >= 2, -ss, ss)
    return cc, ss


def split(v):
    hi = v.astype(BF16)
    lo = (v - hi.astype(F32)).astype(BF16)
    return hi, lo


def stack_table(table):
    hi, lo = split(table)
    return jnp.concatenate([hi, lo, hi], axis=0)


def stack_data(data):
    hi, lo = split(data)
    return jnp.concatenate([hi, hi, lo], axis=1)


def kernel(dims, pot_hbm, mill_ref, mill_smem, pos_ref, aug_hbm, vg_ref, d_ref,
           pot, aug, augf, qall, tx, ty, tz, part, send, recv, phase, kpos, xmid, mixed, dpart, dbuf, dsum,
           pot_sem, aug_sem, s1, r1, own_sem, s2, r2, s3, r3):
    C, ZL, YL, N, S, F, G, SL, PAIRS, ATOMS, ZC, ROWS, PER = dims
    H = ZL // ZC
    ND = F * G
    my_f = lax.axis_index("fft")
    my_g = lax.axis_index("grp")
    me = my_f * G + my_g

    def pot_copy(h, c):
        return pltpu.make_async_copy(
            pot_hbm.at[c, pl.ds(h * ZC, ZC)], pot.at[h, c], pot_sem.at[h, c])

    for h in range(H):
        for c in range(C):
            pot_copy(h, c).start()
    aug_copy = pltpu.make_async_copy(aug_hbm, aug, aug_sem)
    aug_copy.start()

    barrier = pltpu.get_barrier_semaphore()

    def greet(k, _):
        peer = lax.rem(me + k, ND)
        pl.semaphore_signal(barrier, inc=1, device_id={"fft": peer // G, "grp": lax.rem(peer, G)},
                            device_id_type=MESH)
        return 0

    lax.fori_loop(1, ND, greet, 0)

    gx = mill_ref[0:1, :]
    gy = mill_ref[1:2, :]
    cx, sx = cos_sin(lax.broadcasted_iota(jnp.int32, (N, S), 0) * gx, N)
    tx[:, :S] = stack_table(cx)
    tx[:, S:] = stack_table(sx)
    cy, sy = cos_sin((lax.broadcasted_iota(jnp.int32, (YL, S), 0) + my_g * YL) * gy, N)
    ty[0] = cy
    ty[1] = sy

    pl.semaphore_wait(barrier, ND - 1)

    def block_send(h, k):
        peer = lax.rem(me + k, ND)
        pf, pg = peer // G, lax.rem(peer, G)
        return pltpu.make_async_remote_copy(
            src_ref=send.at[h, pf], dst_ref=recv.at[my_g, my_f, h],
            send_sem=s1.at[h, pf * G + pg], recv_sem=r1.at[h, me],
            device_id={"fft": pf, "grp": pg}, device_id_type=MESH)

    def block_recv(h, k):
        peer = lax.rem(me + k, ND)
        pf, pg = peer // G, lax.rem(peer, G)
        return pltpu.make_async_remote_copy(
            src_ref=send.at[h, pf], dst_ref=recv.at[pg, pf, h],
            send_sem=s1.at[h, pf * G + pg], recv_sem=r1.at[h, peer],
            device_id={"fft": pf, "grp": pg}, device_id_type=MESH)

    def group(h, _):
        def component(c, _):
            pot_copy(h, c).wait()
            data = pot[h, c].reshape(ZC * YL, N)
            xmid[...] = jnp.dot(stack_data(data), tx[...], preferred_element_type=F32)
            re_rows = []
            im_rows = []
            for z in range(ZC):
                a = xmid[z * YL:(z + 1) * YL, :S]
                b = xmid[z * YL:(z + 1) * YL, S:]
                re_rows.append(jnp.sum(a * ty[0] - b * ty[1], axis=0, keepdims=True))
                im_rows.append(-jnp.sum(a * ty[1] + b * ty[0], axis=0, keepdims=True))
            part[0, c] = jnp.concatenate(re_rows, axis=0)
            part[1, c] = jnp.concatenate(im_rows, axis=0)
            return 0

        lax.fori_loop(0, C, component, 0)
        for f in range(F):
            pieces = [part[ri, c, :, f * SL:(f + 1) * SL] for ri in range(2) for c in range(C)]
            send[h, f] = jnp.concatenate(pieces, axis=1)

        def start(k, _):
            block_send(h, k).start()
            return 0

        lax.fori_loop(1, ND, start, 0)
        pltpu.make_async_copy(send.at[h, my_f], recv.at[my_g, my_f, h], own_sem.at[h]).start()
        return 0

    lax.fori_loop(0, H, group, 0)

    row = lax.broadcasted_iota(jnp.int32, (N, N), 0)
    col = lax.broadcasted_iota(jnp.int32, (N, N), 1) - N // 2
    cz, sz = cos_sin(row * col, N)
    tz[:, :N] = stack_table(cz)
    tz[:, N:] = stack_table(sz)
    shifted = lax.broadcasted_iota(jnp.int32, (ATOMS, N), 1) - N // 2

    def spread(r):
        rows = jnp.broadcast_to(pos_ref[r:r + 1, :].astype(F32), (ATOMS, ATOMS))
        column = jnp.transpose(rows)[:, 0:1]
        return jnp.broadcast_to(column, (ATOMS, N)).astype(jnp.int32)

    kpos[0] = spread(0)
    kpos[1] = spread(1)
    kpos[2] = spread(2) * shifted

    def phases(s, _):
        gxs = mill_smem[0, my_f * SL + s]
        gys = mill_smem[1, my_f * SL + s]
        cosine, sine = cos_sin(kpos[0] * gxs + kpos[1] * gys + kpos[2], N)
        phase[0, s] = cosine
        phase[1, s] = sine
        return 0

    lax.fori_loop(0, SL, phases, 0)

    aug_copy.wait()
    flat = aug[...].reshape(PAIRS * SL, N)
    for w in range(N // 128):
        augf[w, :PAIRS * SL, :] = flat[:, w * 128:(w + 1) * 128].astype(F32)
        augf[w, PAIRS * SL:, :] = jnp.zeros((ROWS * PER * SL - PAIRS * SL, 128), F32)
    for s in range(SL):
        for w in range(N // 128):
            picked = augf[w, pl.ds(s, ROWS * PER, stride=SL), :]
            qall[:, s * N + w * 128:s * N + (w + 1) * 128] = picked.astype(BF16)

    for h in range(H):
        pltpu.make_async_copy(send.at[h, my_f], recv.at[my_g, my_f, h], own_sem.at[h]).wait()

        def arrive(k, _):
            block_recv(h, k).wait_recv()
            return 0

        lax.fori_loop(1, ND, arrive, 0)

    gathered = recv[0]
    for g in range(1, G):
        gathered = gathered + recv[g]
    lanes = 2 * C * SL
    turned = jnp.transpose(gathered.reshape(F * ZL, lanes))
    pq = jnp.dot(stack_data(turned), tz[...], preferred_element_type=F32)
    half = C * SL
    norm = float(N) ** -1.5
    re = (pq[:half, :N] + pq[half:, N:]) * norm
    im = (pq[half:, :N] - pq[:half, N:]) * norm
    for c in range(C):
        vg_ref[c, 0] = re[c * SL:(c + 1) * SL]
        vg_ref[c, 1] = im[c * SL:(c + 1) * SL]

    my_c, my_j = my_f // PER, lax.rem(my_f, PER)

    def d_send(ci, j):
        owner = ci * PER + j
        return pltpu.make_async_remote_copy(
            src_ref=dpart.at[ci, j], dst_ref=dbuf.at[my_f],
            send_sem=s2.at[owner], recv_sem=r2.at[my_f],
            device_id={"fft": owner}, device_id_type=MESH)

    def contract(i, _):
        ci = lax.rem(my_c + 1 + i, C)
        for s in range(SL):
            vr = vg_ref[ci, 0, s:s + 1, :]
            vi = vg_ref[ci, 1, s:s + 1, :]
            mixed[:, s * N:(s + 1) * N] = (vr * phase[0, s] - vi * phase[1, s]).astype(BF16)
        out = lax.dot_general(qall[...], mixed[...], (((1,), (1,)), ((), ())), preferred_element_type=F32)
        for j in range(PER):
            dpart[ci, j] = out[j * ROWS:(j + 1) * ROWS]
        for j in range(PER):
            @pl.when(ci * PER + j != my_f)
            def _():
                d_send(ci, j).start()
        return 0

    lax.fori_loop(0, C, contract, 0)

    dbuf[my_f] = dpart[my_c, my_j]

    def d_wait(k, _):
        peer = lax.rem(my_f + k, F)
        pltpu.make_async_remote_copy(
            src_ref=dpart.at[peer // PER, lax.rem(peer, PER)], dst_ref=dbuf.at[peer],
            send_sem=s2.at[peer], recv_sem=r2.at[peer],
            device_id={"fft": peer}, device_id_type=MESH).wait_recv()
        return 0

    lax.fori_loop(1, F, d_wait, 0)
    total = dbuf[0]
    for f in range(1, F):
        total = total + dbuf[f]
    dsum[...] = total

    def out_copy(k):
        peer = lax.rem(my_f + k, F)
        return pltpu.make_async_remote_copy(
            src_ref=dsum, dst_ref=d_ref.at[my_c, my_j],
            send_sem=s3.at[peer], recv_sem=r3.at[my_f],
            device_id={"fft": peer}, device_id_type=MESH)

    def out_start(k, _):
        out_copy(k).start()
        return 0

    lax.fori_loop(1, F, out_start, 0)
    d_ref[my_c, my_j] = total

    def drain(k, _):
        for h in range(H):
            block_send(h, k).wait_send()
        return 0

    lax.fori_loop(1, ND, drain, 0)

    def finish(k, _):
        peer = lax.rem(my_f + k, F)
        pf, pj = peer // PER, lax.rem(peer, PER)
        d_send(pf, pj).wait_send()
        out_copy(k).wait_send()
        pltpu.make_async_remote_copy(
            src_ref=dsum, dst_ref=d_ref.at[pf, pj],
            send_sem=s3.at[peer], recv_sem=r3.at[peer],
            device_id={"fft": peer}, device_id_type=MESH).wait_recv()
        return 0

    lax.fori_loop(1, F, finish, 0)


def body(potential, stick_mill, positions, aug_charge):
    C, ZL, YL, N = potential.shape
    S = stick_mill.shape[1]
    F, G = lax.axis_size("fft"), lax.axis_size("grp")
    SL = S // F
    PAIRS = aug_charge.shape[0]
    ATOMS = positions.shape[1]
    ZC = min(8, ZL)
    H = ZL // ZC
    PER = F // C
    ROWS = -(-PAIRS // (PER * 8)) * 8
    ND = F * G
    dims = (C, ZL, YL, N, S, F, G, SL, PAIRS, ATOMS, ZC, ROWS, PER)
    vmem = pl.BlockSpec(memory_space=pltpu.VMEM)
    hbm = pl.BlockSpec(memory_space=pl.ANY)
    dma = pltpu.SemaphoreType.DMA
    vg, d = pl.pallas_call(
        functools.partial(kernel, dims),
        out_shape=(
            jax.ShapeDtypeStruct((C, 2, SL, N), F32),
            jax.ShapeDtypeStruct((C, PER, ROWS, ATOMS), F32),
        ),
        in_specs=[hbm, vmem, pl.BlockSpec(memory_space=pltpu.SMEM), vmem, hbm],
        out_specs=(vmem, vmem),
        scratch_shapes=[
            pltpu.VMEM((H, C, ZC, YL, N), F32),
            pltpu.VMEM((PAIRS, SL, N), BF16),
            pltpu.VMEM((N // 128, ROWS * PER * SL, 128), F32),
            pltpu.VMEM((ROWS * PER, SL * N), BF16),
            pltpu.VMEM((3 * N, 2 * S), BF16),
            pltpu.VMEM((2, YL, S), F32),
            pltpu.VMEM((3 * N, 2 * N), BF16),
            pltpu.VMEM((2, C, ZC, S), F32),
            pltpu.VMEM((H, F, ZC, 2 * C * SL), F32),
            pltpu.VMEM((G, F, H, ZC, 2 * C * SL), F32),
            pltpu.VMEM((2, SL, ATOMS, N), F32),
            pltpu.VMEM((3, ATOMS, N), jnp.int32),
            pltpu.VMEM((ZC * YL, 2 * S), F32),
            pltpu.VMEM((ATOMS, SL * N), BF16),
            pltpu.VMEM((C, PER, ROWS, ATOMS), F32),
            pltpu.VMEM((F, ROWS, ATOMS), F32),
            pltpu.VMEM((ROWS, ATOMS), F32),
            dma((H, C)), dma, dma((H, ND)), dma((H, ND)), dma((H,)),
            dma((F,)), dma((F,)), dma((F,)), dma((F,)),
        ],
        compiler_params=pltpu.CompilerParams(
            collective_id=0, has_side_effects=True, vmem_limit_bytes=60 * 1024 * 1024),
    )(potential, stick_mill, stick_mill, positions, aug_charge)
    return vg, d.reshape(C, PER * ROWS, ATOMS)[:, :PAIRS]


def solution(mesh):
    placed = (P(None, "fft", "grp", None), P(), P(None, "grp"), P(None, "fft", None))
    return jax.shard_map(
        body,
        mesh=mesh,
        in_specs=placed,
        out_specs=(P(None, None, "fft", None), P(None, None, "grp")),
        check_vma=False,
    )
```

```python
import functools
import math

import jax
import jax.numpy as jnp
from jax import lax
from jax.experimental import pallas as pl
from jax.experimental.pallas import tpu as pltpu
from jax.sharding import PartitionSpec as P

MESH = pl.DeviceIdType.MESH
F32 = jnp.float32
BF16 = jnp.bfloat16


def cos_sin(k, n):
    quarter = n // 4
    moved = k + n // 8
    m = jnp.bitwise_and(moved, quarter - 1) - n // 8
    q = jnp.bitwise_and(jnp.right_shift(moved, quarter.bit_length() - 1), 3)
    a = m.astype(F32) * (2.0 * math.pi / n)
    b = a * a
    s = a * (1.0 + b * (-1.0 / 6 + b * (1.0 / 120 + b * (-1.0 / 5040 + b * (1.0 / 362880)))))
    c = 1.0 + b * (-0.5 + b * (1.0 / 24 + b * (-1.0 / 720 + b * (1.0 / 40320))))
    odd = jnp.bitwise_and(q, 1) == 1
    cc = jnp.where(odd, s, c)
    ss = jnp.where(odd, c, s)
    cc = jnp.where((q == 1) | (q == 2), -cc, cc)
    ss = jnp.where(q >= 2, -ss, ss)
    return cc, ss


def split(v):
    hi = v.astype(BF16)
    lo = (v - hi.astype(F32)).astype(BF16)
    return hi, lo


def stack_table(table):
    hi, lo = split(table)
    return jnp.concatenate([hi, lo, hi], axis=0)


def stack_data(data):
    hi, lo = split(data)
    return jnp.concatenate([hi, hi, lo], axis=1)


def kernel(dims, pot_hbm, mill_ref, mill_smem, pos_ref, aug_hbm, vg_ref, d_ref,
           pot, aug, augf, qall, tx, ty, tz, part, send, recv, phase, kpos, xmid, mixed, dpart, dbuf, dsum,
           pot_sem, aug_sem, s1, r1, own_sem, s2, r2, s3, r3):
    C, ZL, YL, N, S, F, G, SL, PAIRS, ATOMS, ZC, ROWS, PER = dims
    H = ZL // ZC
    ND = F * G
    my_f = lax.axis_index("fft")
    my_g = lax.axis_index("grp")
    me = my_f * G + my_g

    def pot_copy(h, c):
        return pltpu.make_async_copy(
            pot_hbm.at[c, pl.ds(h * ZC, ZC)], pot.at[h, c], pot_sem.at[h, c])

    for h in range(H):
        for c in range(C):
            pot_copy(h, c).start()
    aug_copy = pltpu.make_async_copy(aug_hbm, aug, aug_sem)
    aug_copy.start()

    barrier = pltpu.get_barrier_semaphore()

    def greet(k, _):
        peer = lax.rem(me + k, ND)
        pl.semaphore_signal(barrier, inc=1, device_id={"fft": peer // G, "grp": lax.rem(peer, G)},
                            device_id_type=MESH)
        return 0

    lax.fori_loop(1, ND, greet, 0)

    gx = mill_ref[0:1, :]
    gy = mill_ref[1:2, :]
    cx, sx = cos_sin(lax.broadcasted_iota(jnp.int32, (N, S), 0) * gx, N)
    tx[:, :S] = stack_table(cx)
    tx[:, S:] = stack_table(sx)
    cy, sy = cos_sin((lax.broadcasted_iota(jnp.int32, (YL, S), 0) + my_g * YL) * gy, N)
    ty[0] = cy
    ty[1] = sy

    def block_send(h, k):
        peer = lax.rem(me + k, ND)
        pf, pg = peer // G, lax.rem(peer, G)
        return pltpu.make_async_remote_copy(
            src_ref=send.at[h, pf], dst_ref=recv.at[my_g, my_f, h],
            send_sem=s1.at[h, pf * G + pg], recv_sem=r1.at[h, me],
            device_id={"fft": pf, "grp": pg}, device_id_type=MESH)

    def block_recv(h, k):
        peer = lax.rem(me + k, ND)
        pf, pg = peer // G, lax.rem(peer, G)
        return pltpu.make_async_remote_copy(
            src_ref=send.at[h, pf], dst_ref=recv.at[pg, pf, h],
            send_sem=s1.at[h, pf * G + pg], recv_sem=r1.at[h, peer],
            device_id={"fft": pf, "grp": pg}, device_id_type=MESH)

    for h in range(H):
        def component(c, _, h=h):
            pot_copy(h, c).wait()
            data = pot[h, c].reshape(ZC * YL, N)
            xmid[...] = jnp.dot(stack_data(data), tx[...], preferred_element_type=F32)
            re_rows = []
            im_rows = []
            for z in range(ZC):
                a = xmid[z * YL:(z + 1) * YL, :S]
                b = xmid[z * YL:(z + 1) * YL, S:]
                re_rows.append(jnp.sum(a * ty[0] - b * ty[1], axis=0, keepdims=True))
                im_rows.append(-jnp.sum(a * ty[1] + b * ty[0], axis=0, keepdims=True))
            part[0, c] = jnp.concatenate(re_rows, axis=0)
            part[1, c] = jnp.concatenate(im_rows, axis=0)
            return 0

        lax.fori_loop(0, C, component, 0)
        if h == 0:
            pl.semaphore_wait(barrier, ND - 1)
        for f in range(F):
            pieces = [part[ri, c, :, f * SL:(f + 1) * SL] for ri in range(2) for c in range(C)]
            send[h, f] = jnp.concatenate(pieces, axis=1)

        def start(k, _, h=h):
            block_send(h, k).start()
            return 0

        lax.fori_loop(1, ND, start, 0)
        pltpu.make_async_copy(send.at[h, my_f], recv.at[my_g, my_f, h], own_sem.at[h]).start()

    row = lax.broadcasted_iota(jnp.int32, (N, N), 0)
    col = lax.broadcasted_iota(jnp.int32, (N, N), 1) - N // 2
    cz, sz = cos_sin(row * col, N)
    tz[:, :N] = stack_table(cz)
    tz[:, N:] = stack_table(sz)
    shifted = lax.broadcasted_iota(jnp.int32, (ATOMS, N), 1) - N // 2

    def spread(r):
        rows = jnp.broadcast_to(pos_ref[r:r + 1, :].astype(F32), (ATOMS, ATOMS))
        column = jnp.transpose(rows)[:, 0:1]
        return jnp.broadcast_to(column, (ATOMS, N)).astype(jnp.int32)

    kpos[0] = spread(0)
    kpos[1] = spread(1)
    kpos[2] = spread(2) * shifted

    def phases(s, _):
        gxs = mill_smem[0, my_f * SL + s]
        gys = mill_smem[1, my_f * SL + s]
        cosine, sine = cos_sin(kpos[0] * gxs + kpos[1] * gys + kpos[2], N)
        phase[0, s] = cosine
        phase[1, s] = sine
        return 0

    lax.fori_loop(0, SL, phases, 0)

    aug_copy.wait()
    flat = aug[...].reshape(PAIRS * SL, N)
    for w in range(N // 128):
        augf[w, :PAIRS * SL, :] = flat[:, w * 128:(w + 1) * 128].astype(F32)
        augf[w, PAIRS * SL:, :] = jnp.zeros((ROWS * PER * SL - PAIRS * SL, 128), F32)
    for s in range(SL):
        for w in range(N // 128):
            picked = augf[w, pl.ds(s, ROWS * PER, stride=SL), :]
            qall[:, s * N + w * 128:s * N + (w + 1) * 128] = picked.astype(BF16)

    for h in range(H):
        pltpu.make_async_copy(send.at[h, my_f], recv.at[my_g, my_f, h], own_sem.at[h]).wait()

        def arrive(k, _):
            block_recv(h, k).wait_recv()
            return 0

        lax.fori_loop(1, ND, arrive, 0)

    gathered = recv[0]
    for g in range(1, G):
        gathered = gathered + recv[g]
    lanes = 2 * C * SL
    turned = jnp.transpose(gathered.reshape(F * ZL, lanes))
    pq = jnp.dot(stack_data(turned), tz[...], preferred_element_type=F32)
    half = C * SL
    norm = float(N) ** -1.5
    re = (pq[:half, :N] + pq[half:, N:]) * norm
    im = (pq[half:, :N] - pq[:half, N:]) * norm
    for c in range(C):
        vg_ref[c, 0] = re[c * SL:(c + 1) * SL]
        vg_ref[c, 1] = im[c * SL:(c + 1) * SL]

    my_c, my_j = my_f // PER, lax.rem(my_f, PER)

    def d_send(ci, j):
        owner = ci * PER + j
        return pltpu.make_async_remote_copy(
            src_ref=dpart.at[ci, j], dst_ref=dbuf.at[my_f],
            send_sem=s2.at[owner], recv_sem=r2.at[my_f],
            device_id={"fft": owner}, device_id_type=MESH)

    def contract(i, _):
        ci = lax.rem(my_c + 1 + i, C)
        for s in range(SL):
            vr = vg_ref[ci, 0, s:s + 1, :]
            vi = vg_ref[ci, 1, s:s + 1, :]
            mixed[:, s * N:(s + 1) * N] = (vr * phase[0, s] - vi * phase[1, s]).astype(BF16)
        out = lax.dot_general(qall[...], mixed[...], (((1,), (1,)), ((), ())), preferred_element_type=F32)
        for j in range(PER):
            dpart[ci, j] = out[j * ROWS:(j + 1) * ROWS]
        for j in range(PER):
            @pl.when(ci * PER + j != my_f)
            def _():
                d_send(ci, j).start()
        return 0

    lax.fori_loop(0, C, contract, 0)

    dbuf[my_f] = dpart[my_c, my_j]

    def d_wait(k, _):
        peer = lax.rem(my_f + k, F)
        pltpu.make_async_remote_copy(
            src_ref=dpart.at[peer // PER, lax.rem(peer, PER)], dst_ref=dbuf.at[peer],
            send_sem=s2.at[peer], recv_sem=r2.at[peer],
            device_id={"fft": peer}, device_id_type=MESH).wait_recv()
        return 0

    lax.fori_loop(1, F, d_wait, 0)
    total = dbuf[0]
    for f in range(1, F):
        total = total + dbuf[f]
    dsum[...] = total

    def out_copy(k):
        peer = lax.rem(my_f + k, F)
        return pltpu.make_async_remote_copy(
            src_ref=dsum, dst_ref=d_ref.at[my_c, my_j],
            send_sem=s3.at[peer], recv_sem=r3.at[my_f],
            device_id={"fft": peer}, device_id_type=MESH)

    def out_start(k, _):
        out_copy(k).start()
        return 0

    lax.fori_loop(1, F, out_start, 0)
    d_ref[my_c, my_j] = total

    def drain(k, _):
        for h in range(H):
            block_send(h, k).wait_send()
        return 0

    lax.fori_loop(1, ND, drain, 0)

    def finish(k, _):
        peer = lax.rem(my_f + k, F)
        pf, pj = peer // PER, lax.rem(peer, PER)
        d_send(pf, pj).wait_send()
        out_copy(k).wait_send()
        pltpu.make_async_remote_copy(
            src_ref=dsum, dst_ref=d_ref.at[pf, pj],
            send_sem=s3.at[peer], recv_sem=r3.at[peer],
            device_id={"fft": peer}, device_id_type=MESH).wait_recv()
        return 0

    lax.fori_loop(1, F, finish, 0)


def body(potential, stick_mill, positions, aug_charge):
    C, ZL, YL, N = potential.shape
    S = stick_mill.shape[1]
    F, G = lax.axis_size("fft"), lax.axis_size("grp")
    SL = S // F
    PAIRS = aug_charge.shape[0]
    ATOMS = positions.shape[1]
    ZC = min(8, ZL)
    H = ZL // ZC
    PER = F // C
    ROWS = -(-PAIRS // (PER * 8)) * 8
    ND = F * G
    dims = (C, ZL, YL, N, S, F, G, SL, PAIRS, ATOMS, ZC, ROWS, PER)
    vmem = pl.BlockSpec(memory_space=pltpu.VMEM)
    hbm = pl.BlockSpec(memory_space=pl.ANY)
    dma = pltpu.SemaphoreType.DMA
    vg, d = pl.pallas_call(
        functools.partial(kernel, dims),
        out_shape=(
            jax.ShapeDtypeStruct((C, 2, SL, N), F32),
            jax.ShapeDtypeStruct((C, PER, ROWS, ATOMS), F32),
        ),
        in_specs=[hbm, vmem, pl.BlockSpec(memory_space=pltpu.SMEM), vmem, hbm],
        out_specs=(vmem, vmem),
        scratch_shapes=[
            pltpu.VMEM((H, C, ZC, YL, N), F32),
            pltpu.VMEM((PAIRS, SL, N), BF16),
            pltpu.VMEM((N // 128, ROWS * PER * SL, 128), F32),
            pltpu.VMEM((ROWS * PER, SL * N), BF16),
            pltpu.VMEM((3 * N, 2 * S), BF16),
            pltpu.VMEM((2, YL, S), F32),
            pltpu.VMEM((3 * N, 2 * N), BF16),
            pltpu.VMEM((2, C, ZC, S), F32),
            pltpu.VMEM((H, F, ZC, 2 * C * SL), F32),
            pltpu.VMEM((G, F, H, ZC, 2 * C * SL), F32),
            pltpu.VMEM((2, SL, ATOMS, N), F32),
            pltpu.VMEM((3, ATOMS, N), jnp.int32),
            pltpu.VMEM((ZC * YL, 2 * S), F32),
            pltpu.VMEM((ATOMS, SL * N), BF16),
            pltpu.VMEM((C, PER, ROWS, ATOMS), F32),
            pltpu.VMEM((F, ROWS, ATOMS), F32),
            pltpu.VMEM((ROWS, ATOMS), F32),
            dma((H, C)), dma, dma((H, ND)), dma((H, ND)), dma((H,)),
            dma((F,)), dma((F,)), dma((F,)), dma((F,)),
        ],
        compiler_params=pltpu.CompilerParams(
            collective_id=0, has_side_effects=True, vmem_limit_bytes=60 * 1024 * 1024),
    )(potential, stick_mill, stick_mill, positions, aug_charge)
    return vg, d.reshape(C, PER * ROWS, ATOMS)[:, :PAIRS]


def solution(mesh):
    placed = (P(None, "fft", "grp", None), P(), P(None, "grp"), P(None, "fft", None))
    return jax.shard_map(
        body,
        mesh=mesh,
        in_specs=placed,
        out_specs=(P(None, None, "fft", None), P(None, None, "grp")),
        check_vma=False,
    )
```

```python
import functools
import math

import jax
import jax.numpy as jnp
from jax import lax
from jax.experimental import pallas as pl
from jax.experimental.pallas import tpu as pltpu
from jax.sharding import PartitionSpec as P

MESH = pl.DeviceIdType.MESH
F32 = jnp.float32
BF16 = jnp.bfloat16


def cos_sin(k, n):
    quarter = n // 4
    moved = k + n // 8
    m = jnp.bitwise_and(moved, quarter - 1) - n // 8
    q = jnp.bitwise_and(jnp.right_shift(moved, quarter.bit_length() - 1), 3)
    a = m.astype(F32) * (2.0 * math.pi / n)
    b = a * a
    s = a * (1.0 + b * (-1.0 / 6 + b * (1.0 / 120 + b * (-1.0 / 5040 + b * (1.0 / 362880)))))
    c = 1.0 + b * (-0.5 + b * (1.0 / 24 + b * (-1.0 / 720 + b * (1.0 / 40320))))
    odd = jnp.bitwise_and(q, 1) == 1
    cc = jnp.where(odd, s, c)
    ss = jnp.where(odd, c, s)
    cc = jnp.where((q == 1) | (q == 2), -cc, cc)
    ss = jnp.where(q >= 2, -ss, ss)
    return cc, ss


def split(v):
    hi = v.astype(BF16)
    lo = (v - hi.astype(F32)).astype(BF16)
    return hi, lo


def stack_table(table):
    hi, lo = split(table)
    return jnp.concatenate([hi, lo, hi], axis=0)


def stack_data(data):
    hi, lo = split(data)
    return jnp.concatenate([hi, hi, lo], axis=1)


def kernel(dims, pot_hbm, mill_ref, mill_smem, pos_ref, aug_hbm, vg_ref, d_ref,
           pot, aug, augf, qall, tx, ty, tz, part, send, recv, phase, kpos, xmid, mixed, dpart, dbuf, dsum, dfar,
           pot_sem, aug_sem, s1, r1, own_sem, s2, r2, s3, r3, s4, r4, s5, r5):
    C, ZL, YL, N, S, F, G, SL, PAIRS, ATOMS, ZC, ROWS, PER = dims
    H = ZL // ZC
    ND = F * G
    my_f = lax.axis_index("fft")
    my_g = lax.axis_index("grp")
    me = my_f * G + my_g

    def pot_copy(h, c):
        return pltpu.make_async_copy(
            pot_hbm.at[c, pl.ds(h * ZC, ZC)], pot.at[h, c], pot_sem.at[h, c])

    for h in range(H):
        for c in range(C):
            pot_copy(h, c).start()
    aug_copy = pltpu.make_async_copy(aug_hbm, aug, aug_sem)
    aug_copy.start()

    barrier = pltpu.get_barrier_semaphore()

    def greet(k, _):
        peer = lax.rem(me + k, ND)
        pl.semaphore_signal(barrier, inc=1, device_id={"fft": peer // G, "grp": lax.rem(peer, G)},
                            device_id_type=MESH)
        return 0

    lax.fori_loop(1, ND, greet, 0)

    gx = mill_ref[0:1, :]
    gy = mill_ref[1:2, :]
    cx, sx = cos_sin(lax.broadcasted_iota(jnp.int32, (N, S), 0) * gx, N)
    tx[:, :S] = stack_table(cx)
    tx[:, S:] = stack_table(sx)
    cy, sy = cos_sin((lax.broadcasted_iota(jnp.int32, (YL, S), 0) + my_g * YL) * gy, N)
    ty[0] = cy
    ty[1] = sy

    def block_send(h, k):
        peer = lax.rem(me + k, ND)
        pf, pg = peer // G, lax.rem(peer, G)
        return pltpu.make_async_remote_copy(
            src_ref=send.at[h, pf], dst_ref=recv.at[my_g, my_f, h],
            send_sem=s1.at[h, pf * G + pg], recv_sem=r1.at[h, me],
            device_id={"fft": pf, "grp": pg}, device_id_type=MESH)

    def block_recv(h, k):
        peer = lax.rem(me + k, ND)
        pf, pg = peer // G, lax.rem(peer, G)
        return pltpu.make_async_remote_copy(
            src_ref=send.at[h, pf], dst_ref=recv.at[pg, pf, h],
            send_sem=s1.at[h, pf * G + pg], recv_sem=r1.at[h, peer],
            device_id={"fft": pf, "grp": pg}, device_id_type=MESH)

    for h in range(H):
        def component(c, _, h=h):
            pot_copy(h, c).wait()
            data = pot[h, c].reshape(ZC * YL, N)
            xmid[...] = jnp.dot(stack_data(data), tx[...], preferred_element_type=F32)
            re_rows = []
            im_rows = []
            for z in range(ZC):
                a = xmid[z * YL:(z + 1) * YL, :S]
                b = xmid[z * YL:(z + 1) * YL, S:]
                re_rows.append(jnp.sum(a * ty[0] - b * ty[1], axis=0, keepdims=True))
                im_rows.append(-jnp.sum(a * ty[1] + b * ty[0], axis=0, keepdims=True))
            part[0, c] = jnp.concatenate(re_rows, axis=0)
            part[1, c] = jnp.concatenate(im_rows, axis=0)
            return 0

        lax.fori_loop(0, C, component, 0)
        if h == 0:
            pl.semaphore_wait(barrier, ND - 1)
        for f in range(F):
            pieces = [part[ri, c, :, f * SL:(f + 1) * SL] for ri in range(2) for c in range(C)]
            send[h, f] = jnp.concatenate(pieces, axis=1)

        def start(k, _, h=h):
            block_send(h, k).start()
            return 0

        lax.fori_loop(1, ND, start, 0)
        pltpu.make_async_copy(send.at[h, my_f], recv.at[my_g, my_f, h], own_sem.at[h]).start()

    row = lax.broadcasted_iota(jnp.int32, (N, N), 0)
    col = lax.broadcasted_iota(jnp.int32, (N, N), 1) - N // 2
    cz, sz = cos_sin(row * col, N)
    tz[:, :N] = stack_table(cz)
    tz[:, N:] = stack_table(sz)
    shifted = lax.broadcasted_iota(jnp.int32, (ATOMS, N), 1) - N // 2

    def spread(r):
        rows = jnp.broadcast_to(pos_ref[r:r + 1, :].astype(F32), (ATOMS, ATOMS))
        column = jnp.transpose(rows)[:, 0:1]
        return jnp.broadcast_to(column, (ATOMS, N)).astype(jnp.int32)

    kpos[0] = spread(0)
    kpos[1] = spread(1)
    kpos[2] = spread(2) * shifted

    def phases(s, _):
        gxs = mill_smem[0, my_f * SL + s]
        gys = mill_smem[1, my_f * SL + s]
        cosine, sine = cos_sin(kpos[0] * gxs + kpos[1] * gys + kpos[2], N)
        phase[0, s] = cosine
        phase[1, s] = sine
        return 0

    lax.fori_loop(0, SL, phases, 0)

    aug_copy.wait()
    flat = aug[...].reshape(PAIRS * SL, N)
    for w in range(N // 128):
        augf[w, :PAIRS * SL, :] = flat[:, w * 128:(w + 1) * 128].astype(F32)
        augf[w, PAIRS * SL:, :] = jnp.zeros((ROWS * PER * SL - PAIRS * SL, 128), F32)
    for s in range(SL):
        for w in range(N // 128):
            picked = augf[w, pl.ds(s, ROWS * PER, stride=SL), :]
            qall[:, s * N + w * 128:s * N + (w + 1) * 128] = picked.astype(BF16)

    for h in range(H):
        pltpu.make_async_copy(send.at[h, my_f], recv.at[my_g, my_f, h], own_sem.at[h]).wait()

        def arrive(k, _):
            block_recv(h, k).wait_recv()
            return 0

        lax.fori_loop(1, ND, arrive, 0)

    gathered = recv[0]
    for g in range(1, G):
        gathered = gathered + recv[g]
    lanes = 2 * C * SL
    turned = jnp.transpose(gathered.reshape(F * ZL, lanes))
    pq = jnp.dot(stack_data(turned), tz[...], preferred_element_type=F32)
    half = C * SL
    norm = float(N) ** -1.5
    re = (pq[:half, :N] + pq[half:, N:]) * norm
    im = (pq[half:, :N] - pq[:half, N:]) * norm
    for c in range(C):
        vg_ref[c, 0] = re[c * SL:(c + 1) * SL]
        vg_ref[c, 1] = im[c * SL:(c + 1) * SL]

    my_c, my_j = my_f // PER, lax.rem(my_f, PER)

    def line_send(ci, k):
        j = lax.rem(my_j + k, PER)
        return pltpu.make_async_remote_copy(
            src_ref=dpart.at[ci, j], dst_ref=dbuf.at[ci, my_j],
            send_sem=s2.at[ci, j], recv_sem=r2.at[ci, my_j],
            device_id={"fft": my_c * PER + j}, device_id_type=MESH)

    def line_recv(ci, k):
        j = lax.rem(my_j + k, PER)
        return pltpu.make_async_remote_copy(
            src_ref=dpart.at[ci, j], dst_ref=dbuf.at[ci, j],
            send_sem=s2.at[ci, j], recv_sem=r2.at[ci, j],
            device_id={"fft": my_c * PER + j}, device_id_type=MESH)

    def far_copy(k, src, dst, slot, ssem, rsem):
        ci = lax.rem(my_c + k, C)
        return pltpu.make_async_remote_copy(
            src_ref=src, dst_ref=dst, send_sem=ssem.at[ci], recv_sem=rsem.at[slot],
            device_id={"fft": ci * PER + my_j}, device_id_type=MESH)

    def near_copy(ci, k, mine):
        j = lax.rem(my_j + k, PER)
        slot = my_j if mine else j
        return pltpu.make_async_remote_copy(
            src_ref=d_ref.at[ci, slot], dst_ref=d_ref.at[ci, slot],
            send_sem=s5.at[ci, j], recv_sem=r5.at[ci, slot],
            device_id={"fft": my_c * PER + j}, device_id_type=MESH)

    def contract(i, _):
        ci = lax.rem(my_c + 1 + i, C)
        for s in range(SL):
            vr = vg_ref[ci, 0, s:s + 1, :]
            vi = vg_ref[ci, 1, s:s + 1, :]
            mixed[:, s * N:(s + 1) * N] = (vr * phase[0, s] - vi * phase[1, s]).astype(BF16)
        out = lax.dot_general(qall[...], mixed[...], (((1,), (1,)), ((), ())), preferred_element_type=F32)
        for j in range(PER):
            dpart[ci, j] = out[j * ROWS:(j + 1) * ROWS]
        for k in range(1, PER):
            line_send(ci, k).start()
        return 0

    lax.fori_loop(0, C, contract, 0)

    for i in range(C):
        ci = lax.rem(my_c + 1 + i, C)
        dbuf[ci, my_j] = dpart[ci, my_j]
        for k in range(1, PER):
            line_recv(ci, k).wait_recv()
        part_sum = dbuf[ci, 0]
        for j in range(1, PER):
            part_sum = part_sum + dbuf[ci, j]
        dsum[ci] = part_sum
        if i < C - 1:
            far_copy(i + 1, dsum.at[ci], dfar.at[my_c], my_c, s4, r4).start()
        else:
            dfar[my_c] = part_sum
    for k in range(1, C):
        ci = lax.rem(my_c + k, C)
        far_copy(k, dsum.at[ci], dfar.at[ci], ci, s4, r4).wait_recv()
    total = dfar[0]
    for c in range(1, C):
        total = total + dfar[c]
    d_ref[my_c, my_j] = total
    here = d_ref.at[my_c, my_j]
    for k in range(1, C):
        far_copy(k, here, here, my_c, s3, r3).start()
    for k in range(1, PER):
        near_copy(my_c, k, True).start()
    for k in range(1, C):
        ci = lax.rem(my_c + k, C)
        there = d_ref.at[ci, my_j]
        far_copy(k, there, there, ci, s3, r3).wait_recv()
        for n in range(1, PER):
            near_copy(ci, n, True).start()

    def drain(k, _):
        for h in range(H):
            block_send(h, k).wait_send()
        return 0

    lax.fori_loop(1, ND, drain, 0)

    for i in range(C):
        ci = lax.rem(my_c + i, C)
        for k in range(1, PER):
            line_send(ci, k).wait_send()
            near_copy(ci, k, True).wait_send()
            near_copy(ci, k, False).wait_recv()
        if i > 0:
            far_copy(i, dsum.at[ci], dfar.at[my_c], my_c, s4, r4).wait_send()
            far_copy(i, here, here, my_c, s3, r3).wait_send()


def body(potential, stick_mill, positions, aug_charge):
    C, ZL, YL, N = potential.shape
    S = stick_mill.shape[1]
    F, G = lax.axis_size("fft"), lax.axis_size("grp")
    SL = S // F
    PAIRS = aug_charge.shape[0]
    ATOMS = positions.shape[1]
    ZC = min(8, ZL)
    H = ZL // ZC
    PER = F // C
    ROWS = -(-PAIRS // (PER * 8)) * 8
    ND = F * G
    dims = (C, ZL, YL, N, S, F, G, SL, PAIRS, ATOMS, ZC, ROWS, PER)
    vmem = pl.BlockSpec(memory_space=pltpu.VMEM)
    hbm = pl.BlockSpec(memory_space=pl.ANY)
    dma = pltpu.SemaphoreType.DMA
    vg, d = pl.pallas_call(
        functools.partial(kernel, dims),
        out_shape=(
            jax.ShapeDtypeStruct((C, 2, SL, N), F32),
            jax.ShapeDtypeStruct((C, PER, ROWS, ATOMS), F32),
        ),
        in_specs=[hbm, vmem, pl.BlockSpec(memory_space=pltpu.SMEM), vmem, hbm],
        out_specs=(vmem, vmem),
        scratch_shapes=[
            pltpu.VMEM((H, C, ZC, YL, N), F32),
            pltpu.VMEM((PAIRS, SL, N), BF16),
            pltpu.VMEM((N // 128, ROWS * PER * SL, 128), F32),
            pltpu.VMEM((ROWS * PER, SL * N), BF16),
            pltpu.VMEM((3 * N, 2 * S), BF16),
            pltpu.VMEM((2, YL, S), F32),
            pltpu.VMEM((3 * N, 2 * N), BF16),
            pltpu.VMEM((2, C, ZC, S), F32),
            pltpu.VMEM((H, F, ZC, 2 * C * SL), F32),
            pltpu.VMEM((G, F, H, ZC, 2 * C * SL), F32),
            pltpu.VMEM((2, SL, ATOMS, N), F32),
            pltpu.VMEM((3, ATOMS, N), jnp.int32),
            pltpu.VMEM((ZC * YL, 2 * S), F32),
            pltpu.VMEM((ATOMS, SL * N), BF16),
            pltpu.VMEM((C, PER, ROWS, ATOMS), F32),
            pltpu.VMEM((C, PER, ROWS, ATOMS), F32),
            pltpu.VMEM((C, ROWS, ATOMS), F32),
            pltpu.VMEM((C, ROWS, ATOMS), F32),
            dma((H, C)), dma, dma((H, ND)), dma((H, ND)), dma((H,)),
            dma((C, PER)), dma((C, PER)), dma((C,)), dma((C,)),
            dma((C,)), dma((C,)), dma((C, PER)), dma((C, PER)),
        ],
        compiler_params=pltpu.CompilerParams(
            collective_id=0, has_side_effects=True, vmem_limit_bytes=60 * 1024 * 1024),
    )(potential, stick_mill, stick_mill, positions, aug_charge)
    return vg, d.reshape(C, PER * ROWS, ATOMS)[:, :PAIRS]


def solution(mesh):
    placed = (P(None, "fft", "grp", None), P(), P(None, "grp"), P(None, "fft", None))
    return jax.shard_map(
        body,
        mesh=mesh,
        in_specs=placed,
        out_specs=(P(None, None, "fft", None), P(None, None, "grp")),
        check_vma=False,
    )
```
